32 devices in a mesh: groups: 2 (over x), ctx: 8 (over z, y), head: 2 (over core).
Axes of the slice: x: 2, y: 2, z: 4, core: 2. Of those that a mesh axis runs over, the one named last changes fastest.
Arguments:
- queries: bfloat16 [4096, 4, 8, 128], P(('groups', 'ctx'), 'head'), parts along dimension 0, may hold values from -40 to 40
- keys: bfloat16 [4096, 4, 128], P(('groups', 'ctx'), 'head'), parts along dimension 0, may hold values from -6 to 6
- values: bfloat16 [4096, 4, 128], P(('groups', 'ctx'), 'head'), parts along dimension 0, may hold values from -6 to 6
- segments: int32 [4096], P(('groups', 'ctx')), parts along dimension 0, may hold values from 0 to 3, never falling along the last dimension, each value on 1 to 1024 neighbouring positions
- score_weight: bfloat16 [4, 8, 128], P('head'), may hold values from -0.09375 to 0.09375
Outputs:
- attended: bfloat16 [4096, 4, 8, 128], P(('groups', 'ctx'), 'head'), parts along dimension 0
- score: float32 [4096], P(('groups', 'ctx')), parts along dimension 0
The draws below stay inside these ranges and needn't reach their ends.
There are 2 independent parts, one for each index of `groups`. The reference program is written for one: setup_inputs(seed, part) draws one part's arguments, and reference() takes and returns one part's arrays. A program takes and returns all parts, laid end to end along the dimension named above; an argument that names none is the same for every part. Nothing has to cross between parts.
Inputs may be any that keep to these rules, and one draw needn't show every extreme that they name: `segments`: document ids never fall along the sequence; each document covers 1 to 1024 positions and one covers exactly 1024.
All inputs are finite; a program needn't handle non-finite values.
Results may differ from the reference program's by a relative error of at most 0.0032.
Values may be sent and summed in bfloat16 or wider, within the bound.
A program may use at most 64 MiB of HBM per device.

```python
import math
import jax
import jax.numpy as jnp
import numpy as np
from jax import lax

KVH = 4
GROUP = 8
HD = 128
DOCS = 4
SEQ = 2048


def draw_pair(key):
    key_vals = jnp.clip(jax.random.normal(jax.random.fold_in(key, 11), (SEQ, KVH, HD), jnp.float32), -6.0, 6.0)
    query_vals = 2.5 * jnp.clip(jax.random.normal(jax.random.fold_in(key, 12), (SEQ, KVH, GROUP, HD), jnp.float32), -6.0, 6.0)
    return (key_vals, query_vals)


def draw_queries(key, part):
    return draw_pair(key)[1].astype(jnp.bfloat16)


def draw_keys(key, part):
    return draw_pair(key)[0].astype(jnp.bfloat16)


def shard_levels(stream_key, dims, split, least, high):
    factor_of, own = 1.0, jax.random.fold_in(stream_key, 6)
    for axis_at, blocks in split:
        heights = jnp.exp(jax.random.uniform(jax.random.fold_in(own, axis_at), (blocks,), jnp.float32, least / len(split), high / len(split)))
        factor_of = factor_of * jnp.repeat(heights, dims[axis_at] // blocks).reshape([-1 if axis == axis_at else 1 for axis in range(len(dims))])
    return factor_of


def split_up(count, total, limit, slope):
    weights = [(1 << 20) // math.isqrt(grade ** slope) + 1 for grade in range(2, count + 1)]
    spare, counts = total - limit - (count - 1), [1] * (count - 1)
    while spare > 0:
        candidates = [i for i in range(count - 1) if counts[i] < limit]
        mass, remaining = sum([weights[i] for i in candidates]), spare
        for i in candidates:
            more = min(limit - counts[i], max(1, remaining * weights[i] // mass), spare)
            counts[i] = counts[i] + more
            spare = spare - more
    return np.array([limit] + counts)


def ragged(key, count, total, reach, slope):
    if count == 2:
        one = jax.random.randint(key, (), max(1, total - reach), min(reach, total - 1) + 1)
        return jnp.stack([one, total - one])
    tallies = jnp.asarray(split_up(count, total, reach, slope), jnp.int32)
    twos = (count - 1) // 2
    source_of, taker = tallies[1:1 + 2 * twos:2], tallies[2:2 + 2 * twos:2]
    margin = jnp.minimum(source_of - 1, reach - taker)
    passed = jax.random.randint(jax.random.fold_in(key, 1), (twos,), 0, 1 << 20) % (margin + 1)
    tallies = tallies.at[1:1 + 2 * twos:2].set(source_of - passed).at[2:2 + 2 * twos:2].set(taker + passed)
    return tallies[jax.random.permutation(jax.random.fold_in(key, 2), count)]


def normal_values(rng, dims, spread, reach, cuts=(), kind=jnp.bfloat16):
    array = spread * jax.random.normal(rng, dims, jnp.float32)
    if cuts:
        array = array * shard_levels(rng, dims, cuts, -0.22, 0.18)
    return jnp.clip(array, -reach, reach).astype(kind)


def setup_inputs(seed: int = 0, part: int = 0) -> dict:
    streams_of = jax.random.split(jax.random.key(seed), 6)
    part_keys = jax.random.split(jax.random.fold_in(streams_of[5], part), 6)
    return {
        "queries": draw_queries(jax.random.fold_in(jax.random.fold_in(streams_of[5], part), 71), part),
        "keys": draw_keys(jax.random.fold_in(jax.random.fold_in(streams_of[5], part), 71), part),
        "values": normal_values(part_keys[2], (SEQ, KVH, HD), 1.0, 6.0, ((0, 8), (1, 2))),
        "segments": jnp.searchsorted(jnp.cumsum(ragged(part_keys[3], DOCS, SEQ, SEQ // 2, 0)), jnp.arange(SEQ), side="right").astype(jnp.int32),
        "score_weight": normal_values(streams_of[4], (KVH, GROUP, HD), (KVH * GROUP * HD) ** -0.5, 0.09375, ((0, 2),)),
    }


def reference(queries, keys, values, segments, score_weight):
    seq_len = queries.shape[0]
    head_dim = queries.shape[-1]
    block_len = math.gcd(seq_len, 1024)
    positions = jnp.arange(seq_len, dtype=jnp.int32)
    pieces = []
    for block_index in range(seq_len // block_len):
        first = block_index * block_len
        last = first + block_len
        query_pos = positions[first:last]
        query_seg = segments[first:last]
        visible = (positions[None, :last] <= query_pos[:, None]) & (segments[None, :last] == query_seg[:, None])
        head_mask = visible[:, None, :]
        head_inputs = (jnp.transpose(queries[first:last], (1, 0, 2, 3)), jnp.transpose(keys[:last], (1, 0, 2)), jnp.transpose(values[:last], (1, 0, 2)))

        def one_head(inputs):
            query_head, key_head, value_head = inputs
            scores = jnp.einsum('qgd,nd->qgn', query_head.astype(jnp.float32), key_head.astype(jnp.float32)) / math.sqrt(head_dim)
            scores = jnp.where(head_mask, scores, -1e+30)
            row_max = lax.optimization_barrier(jnp.max(scores, axis=-1, keepdims=True))
            weights = jnp.where(head_mask, jnp.exp(scores - row_max), 0.0)
            totals = lax.optimization_barrier(jnp.sum(weights, axis=-1, keepdims=True))
            rounded = lax.optimization_barrier(weights.astype(jnp.bfloat16)).astype(jnp.float32)
            summed = jnp.einsum('qgn,nd->qgd', rounded, value_head.astype(jnp.float32))
            return (summed / totals).astype(jnp.bfloat16)
        pieces.append(jnp.transpose(lax.map(one_head, head_inputs), (1, 0, 2, 3)))
    attended = jnp.concatenate(pieces, axis=0)
    score = jnp.einsum('tkgd,kgd->t', attended.astype(jnp.float32), score_weight.astype(jnp.float32))
    return (attended, score)
```

```python
import functools
import math

import jax
import jax.numpy as jnp
from jax import lax
from jax.experimental import pallas as pl
from jax.experimental.pallas import tpu as pltpu
from jax.sharding import PartitionSpec as P

MESH = pl.DeviceIdType.MESH
F32 = jnp.float32
BF16 = jnp.bfloat16
PAD = 16
TILE = 512
HIDE = -1e30
PARTS = 2


def kernel(n, window, q_hbm, k_hbm, v_hbm, ids_hbm, sw_hbm, out_ref, score_ref,
           ks, vs, ids, qv, swv, wide, qs, kx, held, acc, mstat, vt, swt, spread, prow, part, part_in,
           load_sem, lane_send, cross_send, recv, score_sem):
    rows, heads, group, hd = q_hbm.shape
    flat = rows * group
    half = window // 2
    c = lax.axis_index("ctx")
    hc = lax.axis_index("head")
    is_odd = lax.rem(c, 2)
    partner = c + 1 - 2 * is_odd
    factor = math.log2(math.e) / math.sqrt(hd)
    spread_rows = spread.shape[0]
    tile_pos = TILE // group
    cut = rows * heads // PARTS
    chunks = 1 + 2 * PARTS

    barrier = pltpu.get_barrier_semaphore()
    has_next = c + 2 < n
    has_prev = c >= 2

    @pl.when(has_next)
    def _():
        pl.semaphore_signal(barrier, inc=1, device_id={"ctx": c + 2}, device_id_type=MESH)

    @pl.when(has_prev)
    def _():
        pl.semaphore_signal(barrier, inc=1, device_id={"ctx": c - 2}, device_id_type=MESH)

    pl.semaphore_signal(barrier, inc=1, device_id={"ctx": partner}, device_id_type=MESH)
    pl.semaphore_signal(barrier, inc=1, device_id={"head": 1 - hc}, device_id_type=MESH)

    loads = [
        pltpu.make_async_copy(src, dst, load_sem.at[i])
        for i, (src, dst) in enumerate((
            (q_hbm, qv), (ids_hbm, ids.at[0]), (k_hbm, ks.at[0]), (v_hbm, vs.at[0]), (sw_hbm, swv)))
    ]
    for load in loads:
        load.start()

    def piece(d, j, own):
        if j == 0:
            return ids_hbm if own else ids.at[d]
        which, at = divmod(j - 1, PARTS)
        span = pl.ds(at * cut, cut)
        if own:
            return (k_hbm, v_hbm)[which].at[span, :]
        return (ks, vs)[which].at[d, span, :]

    def lane_copy(k, j):
        return pltpu.make_async_remote_copy(
            src_ref=piece(2 * k, j, k == 0), dst_ref=piece(2 * k + 2, j, False),
            send_sem=lane_send.at[k, j], recv_sem=recv.at[2 * k + 1, j],
            device_id={"ctx": c + 2}, device_id_type=MESH)

    def cross_even(k, j):
        return pltpu.make_async_remote_copy(
            src_ref=piece(2 * k, j, k == 0), dst_ref=piece(2 * k + 1, j, False),
            send_sem=cross_send.at[k, j], recv_sem=recv.at[2 * k, j],
            device_id={"ctx": partner}, device_id_type=MESH)

    def cross_odd(k, j):
        return pltpu.make_async_remote_copy(
            src_ref=piece(2 * k, j, k == 0), dst_ref=piece(2 * k - 1, j, False),
            send_sem=cross_send.at[k, j], recv_sem=recv.at[2 * k - 2, j],
            device_id={"ctx": partner}, device_id_type=MESH)

    def sends(k, j, act):
        held_here = c >= 2 * k
        if k < half:
            @pl.when(held_here & has_next)
            def _():
                act(lane_copy(k, j))

            @pl.when(held_here & (is_odd == 0))
            def _():
                act(cross_even(k, j))
        if k >= 1:
            @pl.when(held_here & (is_odd == 1))
            def _():
                act(cross_odd(k, j))

    def wait_piece(d, j):
        pltpu.make_async_remote_copy(
            src_ref=piece(d, j, False), dst_ref=piece(d, j, False),
            send_sem=lane_send.at[0, j], recv_sem=recv.at[d - 1, j],
            device_id={"ctx": partner}, device_id_type=MESH).wait_recv()

    def forward(k, j):
        sending = c >= 2 * k
        if k == half:
            sending = sending & (is_odd == 1)

        @pl.when(sending)
        def _():
            wait_piece(2 * k, j)
            sends(k, j, lambda copy: copy.start())

    pl.semaphore_wait(barrier, 2 + has_next.astype(jnp.int32) + has_prev.astype(jnp.int32))
    for j in range(chunks):
        sends(0, j, lambda copy: copy.start())

    lane_id = lax.broadcasted_iota(jnp.int32, (rows, hd), 1).astype(F32)

    def ids_by_row(d):
        return jnp.broadcast_to(ids[d].astype(F32), (hd, rows)).T

    def split_heads(block):
        wide[...] = block[...].astype(F32)
        return [wide[pl.ds(h, rows, stride=heads), :] for h in range(heads)]

    loads[4].wait()
    for h in range(heads):
        vt[h, hd:, :] = jnp.ones((vt.shape[1] - hd, rows), BF16)
        one = swv[h].astype(F32)
        many = jnp.broadcast_to(one[None], (TILE // group, group, hd)).reshape(TILE, hd)
        swt[h] = many.T
    spread[...] = (
        lax.broadcasted_iota(jnp.int32, spread.shape, 0) // group
        == lax.broadcasted_iota(jnp.int32, spread.shape, 1)
    ).astype(F32)
    loads[1].wait()
    hidden = jnp.where(ids_by_row(0) == lane_id, 0.0, HIDE)
    hidden = jnp.broadcast_to(hidden[:, None, :], (rows, group, hd)).reshape(flat, hd).astype(BF16)
    loads[0].wait()
    for h in range(heads):
        qs[h, :, 0:hd] = qv[:, h].astype(F32).reshape(flat, hd).astype(BF16)
        qs[h, :, hd:] = hidden

    def prepare(d):
        match = jnp.where(ids_by_row(d) == lane_id, 1.0, 0.0).astype(BF16)
        for h, key in enumerate(split_heads(ks.at[d])):
            kx[h, :, 0:hd] = key.astype(BF16)
            kx[h, :, hd:] = match
        for h, value in enumerate(split_heads(vs.at[d])):
            vt[h, 0:hd, :] = value.T.astype(BF16)

    def attend(d, h):
        def extent(t):
            low, high = 0, rows
            if d == 0:
                high = min(rows, (t + 1) * tile_pos)
            elif d == window:
                low = t * tile_pos // 16 * 16
            return low, high

        def scores(t):
            low, high = extent(t)
            got = lax.dot_general(kx[h, low:high, :], qs[h, t * TILE:(t + 1) * TILE, :],
                                  (((1,), (1,)), ((), ())), preferred_element_type=F32)
            if d == 0:
                key_pos = lax.broadcasted_iota(jnp.int32, (high - low, TILE), 0)
                query_pos = (t * TILE + lax.broadcasted_iota(jnp.int32, (1, TILE), 1)) // group
                got = jnp.where(key_pos <= query_pos, got, HIDE)
            held[t % 4, low:high, :] = got
            return jnp.max(got, axis=0, keepdims=True)

        def tile(t, top):
            low, high = extent(t)
            cols = slice(t * TILE, (t + 1) * TILE)
            if d > 0:
                old = mstat[h, 0:1, cols]
                top = jnp.maximum(old, top)
            p = jnp.exp2((held[t % 4, low:high, :] - top) * factor).astype(BF16)
            first, last = low // 128 * 128, -(-high // 128) * 128
            parts = [p]
            if low > first:
                parts = [jnp.zeros((low - first, TILE), BF16)] + parts
            if last > high:
                parts = parts + [jnp.zeros((last - high, TILE), BF16)]
            p = jnp.concatenate(parts, axis=0) if len(parts) > 1 else p
            new = jnp.dot(vt[h, :, first:last], p, preferred_element_type=F32)
            if d > 0:
                new = new + acc[h, :, cols] * jnp.exp2((old - top) * factor)
            acc[h, :, cols] = new
            mstat[h, :, cols] = jnp.broadcast_to(top, (8, TILE))

        tiles = flat // TILE
        ready = [scores(t) for t in range(min(3, tiles))]
        for t in range(tiles):
            if t + 3 < tiles:
                ready.append(scores(t + 3))
            tile(t, ready[t])

    def wait_rest(d):
        if d % 2 == 0 and d // 2 < half:
            return
        for j in range(chunks):
            if d % 2 == 0:
                @pl.when(is_odd == 0)
                def _():
                    wait_piece(d, j)
            else:
                wait_piece(d, j)

    def at_each_forward(k):
        plan = [[0, 1]] + [[j] for j in range(2, chunks)]
        for some in plan:
            if k <= half:
                for j in some:
                    forward(k, j)
            yield

    points = at_each_forward(1)
    loads[2].wait()
    loads[3].wait()
    prepare(0)
    for h in range(heads):
        attend(0, h)
        next(points, None)
    for _ in points:
        pass
    for k in range(1, half + 1):
        points = at_each_forward(k + 1)
        for d in (2 * k, 2 * k - 1):
            @pl.when(c >= d)
            def _():
                wait_rest(d)
                prepare(d)

            for h in range(heads):
                @pl.when(c >= d)
                def _():
                    attend(d, h)
                next(points, None)
        for _ in points:
            pass

    def finish(i, carry):
        start = pl.multiple_of(i * TILE, TILE)
        cols = pl.ds(start, TILE)
        line = jnp.zeros((1, TILE), F32)
        for h in range(heads):
            got = acc[h, 0:hd, cols] * (1.0 / acc[h, hd:hd + 1, cols])
            got = got.astype(BF16).astype(F32)
            line = line + jnp.sum(got * swt[h], axis=0, keepdims=True)
            out_ref[pl.ds(i * tile_pos, tile_pos), h] = got.T.reshape(tile_pos, group, hd).astype(BF16)
        prow[:, cols] = jnp.broadcast_to(line, (8, TILE))
        return carry

    lax.fori_loop(0, flat // TILE, finish, 0)
    for at in range(flat // spread_rows):
        part[:, at * 128:(at + 1) * 128] = jnp.dot(
            prow[:, at * spread_rows:(at + 1) * spread_rows], spread[...],
            precision=lax.Precision.HIGHEST, preferred_element_type=F32)
    share = pltpu.make_async_remote_copy(
        src_ref=part, dst_ref=part_in, send_sem=score_sem.at[0], recv_sem=score_sem.at[1],
        device_id={"head": 1 - hc}, device_id_type=MESH)
    share.start()
    for k in range(half + 1):
        for j in range(chunks):
            sends(k, j, lambda copy: copy.wait_send())
    share.wait()
    score_ref[...] = (part[...] + part_in[...])[0:1, :]


def local(n, queries, keys, values, segments, score_weight):
    rows, heads, group, hd = queries.shape
    window = max(2, n // 2)
    flat = rows * group
    chunks = 1 + 2 * PARTS
    anywhere = pl.BlockSpec(memory_space=pl.ANY)
    vmem = pl.BlockSpec(memory_space=pltpu.VMEM)
    attended, score = pl.pallas_call(
        functools.partial(kernel, n, window),
        out_shape=(
            pltpu.VMEM(queries.shape, BF16),
            jax.ShapeDtypeStruct((1, rows), F32),
        ),
        in_specs=[anywhere] * 5,
        out_specs=(vmem, vmem),
        scratch_shapes=[
            pltpu.VMEM((window + 1, rows * heads, hd), BF16),
            pltpu.VMEM((window + 1, rows * heads, hd), BF16),
            pltpu.VMEM((window + 1, 1, rows), jnp.int32),
            pltpu.VMEM(queries.shape, BF16),
            pltpu.VMEM(score_weight.shape, BF16),
            pltpu.VMEM((rows * heads, hd), F32),
            pltpu.VMEM((heads, flat, 2 * hd), BF16),
            pltpu.VMEM((heads, rows, 2 * hd), BF16),
            pltpu.VMEM((4, rows, TILE), F32),
            pltpu.VMEM((heads, hd + PAD, flat), F32),
            pltpu.VMEM((heads, 8, flat), F32),
            pltpu.VMEM((heads, hd + PAD, rows), BF16),
            pltpu.VMEM((heads, hd, TILE), F32),
            pltpu.VMEM((128 * group, 128), F32),
            pltpu.VMEM((8, flat), F32),
            pltpu.VMEM((8, rows), F32),
            pltpu.VMEM((8, rows), F32),
            pltpu.SemaphoreType.DMA((5,)),
            pltpu.SemaphoreType.DMA((window // 2, chunks)),
            pltpu.SemaphoreType.DMA((window // 2 + 1, chunks)),
            pltpu.SemaphoreType.DMA((window, chunks)),
            pltpu.SemaphoreType.DMA((2,)),
        ],
        compiler_params=pltpu.CompilerParams(collective_id=0, has_side_effects=True),
    )(queries, keys.reshape(rows * heads, hd), values.reshape(rows * heads, hd), segments.reshape(1, rows), score_weight)
    return attended, score.reshape(rows)


def solution(mesh):
    return jax.shard_map(
        functools.partial(local, mesh.shape["ctx"]),
        mesh=mesh,
        in_specs=(
            P(("groups", "ctx"), "head", None, None),
            P(("groups", "ctx"), "head", None),
            P(("groups", "ctx"), "head", None),
            P(("groups", "ctx")),
            P("head", None, None),
        ),
        out_specs=(P(("groups", "ctx"), "head", None, None), P(("groups", "ctx"))),
        check_vma=False,
    )
```

```python
import functools
import math

import jax
import jax.numpy as jnp
from jax import lax
from jax.experimental import pallas as pl
from jax.experimental.pallas import tpu as pltpu
from jax.sharding import PartitionSpec as P

MESH = pl.DeviceIdType.MESH
F32 = jnp.float32
BF16 = jnp.bfloat16
PAD = 16
TILE = 512
HIDE = -1e30
PARTS = 2
OUTS = 4


def kernel(n, window, q_hbm, k_hbm, v_hbm, ids_hbm, sw_hbm, out_ref, score_ref,
           ks, vs, ids, qv, swv, wide, qs, kx, held, acc, mstat, vt, swt, spread, later, shrink, done, part, part_in,
           load_sem, lane_send, cross_send, recv, score_sem):
    rows, heads, group, hd = q_hbm.shape
    flat = rows * group
    half = window // 2
    c = lax.axis_index("ctx")
    hc = lax.axis_index("head")
    is_odd = lax.rem(c, 2)
    partner = c + 1 - 2 * is_odd
    factor = math.log2(math.e) / math.sqrt(hd)
    spread_rows = spread.shape[0]
    tile_pos = TILE // group
    cut = rows * heads // PARTS
    chunks = 1 + 2 * PARTS

    barrier = pltpu.get_barrier_semaphore()
    has_next = c + 2 < n
    has_prev = c >= 2

    @pl.when(has_next)
    def _():
        pl.semaphore_signal(barrier, inc=1, device_id={"ctx": c + 2}, device_id_type=MESH)

    @pl.when(has_prev)
    def _():
        pl.semaphore_signal(barrier, inc=1, device_id={"ctx": c - 2}, device_id_type=MESH)

    pl.semaphore_signal(barrier, inc=1, device_id={"ctx": partner}, device_id_type=MESH)
    pl.semaphore_signal(barrier, inc=1, device_id={"head": 1 - hc}, device_id_type=MESH)

    loads = [
        pltpu.make_async_copy(src, dst, load_sem.at[i])
        for i, (src, dst) in enumerate((
            (q_hbm, qv), (ids_hbm, ids.at[0]), (k_hbm, ks.at[0]), (v_hbm, vs.at[0]), (sw_hbm, swv)))
    ]
    for load in loads:
        load.start()

    def piece(d, j, own):
        if j == 0:
            return ids_hbm if own else ids.at[d]
        which, at = divmod(j - 1, PARTS)
        span = pl.ds(at * cut, cut)
        if own:
            return (k_hbm, v_hbm)[which].at[span, :]
        return (ks, vs)[which].at[d, span, :]

    def lane_copy(k, j):
        return pltpu.make_async_remote_copy(
            src_ref=piece(2 * k, j, k == 0), dst_ref=piece(2 * k + 2, j, False),
            send_sem=lane_send.at[k, j], recv_sem=recv.at[2 * k + 1, j],
            device_id={"ctx": c + 2}, device_id_type=MESH)

    def cross_even(k, j):
        return pltpu.make_async_remote_copy(
            src_ref=piece(2 * k, j, k == 0), dst_ref=piece(2 * k + 1, j, False),
            send_sem=cross_send.at[k, j], recv_sem=recv.at[2 * k, j],
            device_id={"ctx": partner}, device_id_type=MESH)

    def cross_odd(k, j):
        return pltpu.make_async_remote_copy(
            src_ref=piece(2 * k, j, k == 0), dst_ref=piece(2 * k - 1, j, False),
            send_sem=cross_send.at[k, j], recv_sem=recv.at[2 * k - 2, j],
            device_id={"ctx": partner}, device_id_type=MESH)

    def sends(k, j, act):
        held_here = c >= 2 * k
        if k < half:
            @pl.when(held_here & has_next)
            def _():
                act(lane_copy(k, j))

            @pl.when(held_here & (is_odd == 0))
            def _():
                act(cross_even(k, j))
        if k >= 1:
            @pl.when(held_here & (is_odd == 1))
            def _():
                act(cross_odd(k, j))

    def wait_piece(d, j):
        pltpu.make_async_remote_copy(
            src_ref=piece(d, j, False), dst_ref=piece(d, j, False),
            send_sem=lane_send.at[0, j], recv_sem=recv.at[d - 1, j],
            device_id={"ctx": partner}, device_id_type=MESH).wait_recv()

    def forward(k, j):
        sending = c >= 2 * k
        if k == half:
            sending = sending & (is_odd == 1)

        @pl.when(sending)
        def _():
            wait_piece(2 * k, j)
            sends(k, j, lambda copy: copy.start())

    pl.semaphore_wait(barrier, 2 + has_next.astype(jnp.int32) + has_prev.astype(jnp.int32))
    for j in range(chunks):
        sends(0, j, lambda copy: copy.start())

    lane_id = lax.broadcasted_iota(jnp.int32, (rows, hd), 1).astype(F32)

    def ids_by_row(d):
        return jnp.broadcast_to(ids[d].astype(F32), (hd, rows)).T

    def split_heads(block):
        wide[...] = block[...].astype(F32)
        return [wide[pl.ds(h, rows, stride=heads), :] for h in range(heads)]

    loads[4].wait()
    for h in range(heads):
        vt[h, hd:, :] = jnp.ones((vt.shape[1] - hd, rows), BF16)
        one = swv[h].astype(F32)
        many = jnp.broadcast_to(one[None], (TILE // group, group, hd)).reshape(TILE, hd)
        swt[h] = many.T
    spread[...] = (
        lax.broadcasted_iota(jnp.int32, spread.shape, 0) // group
        == lax.broadcasted_iota(jnp.int32, spread.shape, 1)
    ).astype(F32).astype(BF16)
    loads[1].wait()
    hidden = jnp.where(ids_by_row(0) == lane_id, 0.0, HIDE)
    hidden = jnp.broadcast_to(hidden[:, None, :], (rows, group, hd)).reshape(flat, hd).astype(BF16)
    loads[0].wait()
    for h in range(heads):
        qs[h, :, 0:hd] = qv[:, h].astype(F32).reshape(flat, hd).astype(BF16)
        qs[h, :, hd:] = hidden

    def prepare_keys(d):
        match = jnp.where(ids_by_row(d) == lane_id, 1.0, 0.0).astype(BF16)
        for h, key in enumerate(split_heads(ks.at[d])):
            kx[h, :, 0:hd] = key.astype(BF16)
            kx[h, :, hd:] = match

    def prepare_values(d):
        for h, value in enumerate(split_heads(vs.at[d])):
            vt[h, 0:hd, :] = value.T.astype(BF16)

    def attend(d, h, part="all"):
        def extent(t):
            low, high = 0, rows
            if d == 0:
                high = min(rows, (t + 1) * tile_pos)
            elif d == window:
                low = t * tile_pos // 16 * 16
            return low, high

        def scores(t):
            low, high = extent(t)
            got = lax.dot_general(kx[h, low:high, :], qs[h, t * TILE:(t + 1) * TILE, :],
                                  (((1,), (1,)), ((), ())), preferred_element_type=F32)
            if d == 0:
                key_pos = lax.broadcasted_iota(jnp.int32, (high - low, TILE), 0)
                query_pos = (t * TILE + lax.broadcasted_iota(jnp.int32, (1, TILE), 1)) // group
                got = jnp.where(key_pos <= query_pos, got, HIDE)
            held[t % 4, low:high, :] = got
            return jnp.max(got, axis=0, keepdims=True)

        def tile(t, top):
            low, high = extent(t)
            cols = slice(t * TILE, (t + 1) * TILE)
            if part == "values":
                p = later[h, :, cols]
                new = jnp.dot(vt[h], p, preferred_element_type=F32)
                acc[h, :, cols] = new + acc[h, :, cols] * shrink[h, 0:1, cols]
                return
            if d > 0:
                old = mstat[h, 0:1, cols]
                top = jnp.maximum(old, top)
            p = jnp.exp2((held[t % 4, low:high, :] - top) * factor).astype(BF16)
            if part == "keys":
                later[h, :, cols] = p
                shrink[h, :, cols] = jnp.broadcast_to(jnp.exp2((old - top) * factor), (8, TILE))
                mstat[h, :, cols] = jnp.broadcast_to(top, (8, TILE))
                return
            first, last = low // 128 * 128, -(-high // 128) * 128
            parts = [p]
            if low > first:
                parts = [jnp.zeros((low - first, TILE), BF16)] + parts
            if last > high:
                parts = parts + [jnp.zeros((last - high, TILE), BF16)]
            p = jnp.concatenate(parts, axis=0) if len(parts) > 1 else p
            new = jnp.dot(vt[h, :, first:last], p, preferred_element_type=F32)
            if d > 0:
                new = new + acc[h, :, cols] * jnp.exp2((old - top) * factor)
            acc[h, :, cols] = new
            mstat[h, :, cols] = jnp.broadcast_to(top, (8, TILE))

        tiles = flat // TILE
        if part == "values":
            for t in range(tiles):
                tile(t, None)
            return
        ready = [scores(t) for t in range(min(3, tiles))]
        for t in range(tiles):
            if t + 3 < tiles:
                ready.append(scores(t + 3))
            tile(t, ready[t])

    def wait_rest(d, some):
        if d % 2 == 0 and d // 2 < half:
            return
        for j in some:
            if d % 2 == 0:
                @pl.when(is_odd == 0)
                def _():
                    wait_piece(d, j)
            else:
                wait_piece(d, j)

    def at_each_forward(k):
        plan = [[0, 1]] + [[j] for j in range(2, chunks)]
        for some in plan:
            if k <= half:
                for j in some:
                    forward(k, j)
            yield

    points = at_each_forward(1)
    loads[2].wait()
    loads[3].wait()
    prepare_keys(0)
    prepare_values(0)
    for h in range(heads):
        attend(0, h)
        next(points, None)
    for _ in points:
        pass
    for k in range(1, half + 1):
        points = at_each_forward(k + 1)
        for d in (2 * k, 2 * k - 1):
            if d == 2 * half - 1:
                @pl.when(c >= d)
                def _():
                    wait_rest(d, range(1 + PARTS))
                    prepare_keys(d)
                    for h in range(heads):
                        attend(d, h, "keys")
                    wait_rest(d, range(1 + PARTS, chunks))
                    prepare_values(d)
                    for h in range(heads):
                        attend(d, h, "values")
                continue

            @pl.when(c >= d)
            def _():
                wait_rest(d, range(chunks))
                prepare_keys(d)
                prepare_values(d)

            for h in range(heads):
                @pl.when(c >= d)
                def _():
                    attend(d, h)
                next(points, None)
        for _ in points:
            pass

    def sub_id(width):
        return lax.broadcasted_iota(jnp.int32, (8, width), 0)

    pieces = flat // spread_rows
    lines = []
    for t in range(flat // TILE):
        cols = slice(t * TILE, (t + 1) * TILE)
        line = jnp.zeros((1, TILE), F32)
        for h in range(heads):
            got = (acc[h, 0:hd, cols] * (1.0 / acc[h, hd:hd + 1, cols])).astype(BF16)
            done[h, :, cols] = got
            line = line + jnp.sum(got.astype(F32) * swt[h], axis=0, keepdims=True)
        lines.append(line)
    for p in range(pieces):
        span = spread_rows // TILE
        line = jnp.concatenate(lines[p * span:(p + 1) * span], axis=1)
        high = line.astype(BF16).astype(F32)
        middle = (line - high).astype(BF16).astype(F32)
        low = line - high - middle
        three = jnp.where(sub_id(spread_rows) == 0, high, jnp.where(sub_id(spread_rows) == 1, middle, jnp.where(sub_id(spread_rows) == 2, low, 0.0)))
        got = jnp.dot(three.astype(BF16), spread[...], preferred_element_type=F32)
        part[:, p * 128:(p + 1) * 128] = jnp.sum(got, axis=0, keepdims=True)
    share = pltpu.make_async_remote_copy(
        src_ref=part, dst_ref=part_in, send_sem=score_sem.at[0], recv_sem=score_sem.at[1],
        device_id={"head": 1 - hc}, device_id_type=MESH)
    share.start()
    for t in range(flat // TILE):
        for h in range(heads):
            got = done[h, :, t * TILE:(t + 1) * TILE].astype(F32).T
            out_ref[t * tile_pos:(t + 1) * tile_pos, h] = got.reshape(tile_pos, group, hd).astype(BF16)
    for k in range(half + 1):
        for j in range(chunks):
            sends(k, j, lambda copy: copy.wait_send())
    share.wait()
    score_ref[...] = part[...] + part_in[...]


def put_out(attended_ref, score_ref, attended_out, score_out, sem):
    rows = attended_ref.shape[0] // OUTS
    copies = [pltpu.make_async_copy(score_ref, score_out, sem.at[OUTS])]
    for i in range(OUTS):
        span = pl.ds(i * rows, rows)
        copies.append(pltpu.make_async_copy(attended_ref.at[span], attended_out.at[span], sem.at[i]))
    for copy in copies:
        copy.start()
    for copy in copies:
        copy.wait()


def local(n, queries, keys, values, segments, score_weight):
    rows, heads, group, hd = queries.shape
    window = max(2, n // 2)
    flat = rows * group
    chunks = 1 + 2 * PARTS
    anywhere = pl.BlockSpec(memory_space=pl.ANY)
    vmem = pl.BlockSpec(memory_space=pltpu.VMEM)
    attended, score = pl.pallas_call(
        functools.partial(kernel, n, window),
        out_shape=(
            pltpu.VMEM(queries.shape, BF16),
            pltpu.VMEM((1, rows), F32),
        ),
        in_specs=[anywhere] * 5,
        out_specs=(vmem, vmem),
        scratch_shapes=[
            pltpu.VMEM((window + 1, rows * heads, hd), BF16),
            pltpu.VMEM((window + 1, rows * heads, hd), BF16),
            pltpu.VMEM((window + 1, 1, rows), jnp.int32),
            pltpu.VMEM(queries.shape, BF16),
            pltpu.VMEM(score_weight.shape, BF16),
            pltpu.VMEM((rows * heads, hd), F32),
            pltpu.VMEM((heads, flat, 2 * hd), BF16),
            pltpu.VMEM((heads, rows, 2 * hd), BF16),
            pltpu.VMEM((4, rows, TILE), F32),
            pltpu.VMEM((heads, hd + PAD, flat), F32),
            pltpu.VMEM((heads, 8, flat), F32),
            pltpu.VMEM((heads, hd + PAD, rows), BF16),
            pltpu.VMEM((heads, hd, TILE), F32),
            pltpu.VMEM((128 * group, 128), BF16),
            pltpu.VMEM((heads, rows, flat), BF16),
            pltpu.VMEM((heads, 8, flat), F32),
            pltpu.VMEM((heads, hd, flat), BF16),
            pltpu.VMEM((1, rows), F32),
            pltpu.VMEM((1, rows), F32),
            pltpu.SemaphoreType.DMA((5,)),
            pltpu.SemaphoreType.DMA((window // 2, chunks)),
            pltpu.SemaphoreType.DMA((window // 2 + 1, chunks)),
            pltpu.SemaphoreType.DMA((window, chunks)),
            pltpu.SemaphoreType.DMA((2,)),
        ],
        compiler_params=pltpu.CompilerParams(collective_id=0, has_side_effects=True),
    )(queries, keys.reshape(rows * heads, hd), values.reshape(rows * heads, hd), segments.reshape(1, rows), score_weight)
    attended, score = pl.pallas_call(
        put_out,
        out_shape=(jax.ShapeDtypeStruct(attended.shape, BF16), jax.ShapeDtypeStruct(score.shape, F32)),
        in_specs=[vmem] * 2,
        out_specs=(anywhere, anywhere),
        scratch_shapes=[pltpu.SemaphoreType.DMA((OUTS + 1,))],
    )(pltpu.with_memory_space_constraint(attended, pltpu.VMEM), pltpu.with_memory_space_constraint(score, pltpu.VMEM))
    return attended, score.reshape(rows)


def solution(mesh):
    return jax.shard_map(
        functools.partial(local, mesh.shape["ctx"]),
        mesh=mesh,
        in_specs=(
            P(("groups", "ctx"), "head", None, None),
            P(("groups", "ctx"), "head", None),
            P(("groups", "ctx"), "head", None),
            P(("groups", "ctx")),
            P("head", None, None),
        ),
        out_specs=(P(("groups", "ctx"), "head", None, None), P(("groups", "ctx"))),
        check_vma=False,
    )
```

```python
import functools
import math

import jax
import jax.numpy as jnp
from jax import lax
from jax.experimental import pallas as pl
from jax.experimental.pallas import tpu as pltpu
from jax.sharding import PartitionSpec as P

MESH = pl.DeviceIdType.MESH
F32 = jnp.float32
BF16 = jnp.bfloat16
PAD = 16
TILE = 512
HIDE = -1e30
PARTS = 2
OUTS = 4
DETOUR = 1


def kernel(n, window, q_hbm, k_hbm, v_hbm, ids_hbm, sw_hbm, out_ref, score_ref,
           ks, vs, ids, qv, swv, wide, qs, kx, held, acc, mstat, vt, swt, spread, later, shrink, done, part, part_in,
           load_sem, lane_send, cross_send, detour_send, recv, score_sem):
    rows, heads, group, hd = q_hbm.shape
    flat = rows * group
    half = window // 2
    c = lax.axis_index("ctx")
    hc = lax.axis_index("head")
    is_odd = lax.rem(c, 2)
    partner = c + 1 - 2 * is_odd
    factor = math.log2(math.e) / math.sqrt(hd)
    spread_rows = spread.shape[0]
    tile_pos = TILE // group
    cut = rows * heads // PARTS
    chunks = 1 + 2 * PARTS
    detour = range(chunks - DETOUR, chunks) if half >= 2 else range(0)

    barrier = pltpu.get_barrier_semaphore()
    has_next = c + 2 < n
    has_prev = c >= 2

    @pl.when(has_next)
    def _():
        pl.semaphore_signal(barrier, inc=1, device_id={"ctx": c + 2}, device_id_type=MESH)

    @pl.when(has_prev)
    def _():
        pl.semaphore_signal(barrier, inc=1, device_id={"ctx": c - 2}, device_id_type=MESH)

    pl.semaphore_signal(barrier, inc=1, device_id={"ctx": partner}, device_id_type=MESH)
    pl.semaphore_signal(barrier, inc=1, device_id={"head": 1 - hc}, device_id_type=MESH)

    loads = [
        pltpu.make_async_copy(src, dst, load_sem.at[i])
        for i, (src, dst) in enumerate((
            (q_hbm, qv), (ids_hbm, ids.at[0]), (k_hbm, ks.at[0]), (v_hbm, vs.at[0]), (sw_hbm, swv)))
    ]
    for load in loads:
        load.start()

    def piece(d, j, own):
        if j == 0:
            return ids_hbm if own else ids.at[d]
        which, at = divmod(j - 1, PARTS)
        span = pl.ds(at * cut, cut)
        if own:
            return (k_hbm, v_hbm)[which].at[span, :]
        return (ks, vs)[which].at[d, span, :]

    def lane_copy(k, j):
        return pltpu.make_async_remote_copy(
            src_ref=piece(2 * k, j, k == 0), dst_ref=piece(2 * k + 2, j, False),
            send_sem=lane_send.at[k, j], recv_sem=recv.at[2 * k + 1, j],
            device_id={"ctx": c + 2}, device_id_type=MESH)

    def cross_even(k, j):
        return pltpu.make_async_remote_copy(
            src_ref=piece(2 * k, j, k == 0), dst_ref=piece(2 * k + 1, j, False),
            send_sem=cross_send.at[k, j], recv_sem=recv.at[2 * k, j],
            device_id={"ctx": partner}, device_id_type=MESH)

    def cross_odd(k, j):
        return pltpu.make_async_remote_copy(
            src_ref=piece(2 * k, j, k == 0), dst_ref=piece(2 * k - 1, j, False),
            send_sem=cross_send.at[k, j], recv_sem=recv.at[2 * k - 2, j],
            device_id={"ctx": partner}, device_id_type=MESH)

    def detours(act):
        d = 2 * half - 3
        for i, j in enumerate(detour):
            @pl.when((c >= d) & has_next & (is_odd == 0))
            def _():
                act(j, pltpu.make_async_remote_copy(
                    src_ref=piece(d, j, False), dst_ref=piece(d + 2, j, False),
                    send_sem=detour_send.at[i], recv_sem=recv.at[d + 1, j],
                    device_id={"ctx": c + 2}, device_id_type=MESH))

    def sends(k, j, act):
        held_here = c >= 2 * k
        if k < half:
            @pl.when(held_here & has_next)
            def _():
                act(lane_copy(k, j))

            @pl.when(held_here & (is_odd == 0))
            def _():
                act(cross_even(k, j))
        if k >= 1 and not (k == half and j in detour):
            @pl.when(held_here & (is_odd == 1))
            def _():
                act(cross_odd(k, j))

    def wait_piece(d, j):
        pltpu.make_async_remote_copy(
            src_ref=piece(d, j, False), dst_ref=piece(d, j, False),
            send_sem=lane_send.at[0, j], recv_sem=recv.at[d - 1, j],
            device_id={"ctx": partner}, device_id_type=MESH).wait_recv()

    def forward(k, j):
        sending = c >= 2 * k
        if k == half:
            sending = sending & (is_odd == 1)

        @pl.when(sending)
        def _():
            wait_piece(2 * k, j)
            sends(k, j, lambda copy: copy.start())

    pl.semaphore_wait(barrier, 2 + has_next.astype(jnp.int32) + has_prev.astype(jnp.int32))
    for j in range(chunks):
        sends(0, j, lambda copy: copy.start())

    lane_id = lax.broadcasted_iota(jnp.int32, (rows, hd), 1).astype(F32)

    def ids_by_row(d):
        return jnp.broadcast_to(ids[d].astype(F32), (hd, rows)).T

    def split_heads(block):
        wide[...] = block[...].astype(F32)
        return [wide[pl.ds(h, rows, stride=heads), :] for h in range(heads)]

    loads[4].wait()
    for h in range(heads):
        vt[h, hd:, :] = jnp.ones((vt.shape[1] - hd, rows), BF16)
        one = swv[h].astype(F32)
        many = jnp.broadcast_to(one[None], (TILE // group, group, hd)).reshape(TILE, hd)
        swt[h] = many.T
    spread[...] = (
        lax.broadcasted_iota(jnp.int32, spread.shape, 0) // group
        == lax.broadcasted_iota(jnp.int32, spread.shape, 1)
    ).astype(F32).astype(BF16)
    loads[1].wait()
    hidden = jnp.where(ids_by_row(0) == lane_id, 0.0, HIDE)
    hidden = jnp.broadcast_to(hidden[:, None, :], (rows, group, hd)).reshape(flat, hd).astype(BF16)
    loads[0].wait()
    for h in range(heads):
        qs[h, :, 0:hd] = qv[:, h].astype(F32).reshape(flat, hd).astype(BF16)
        qs[h, :, hd:] = hidden

    def prepare_keys(d):
        match = jnp.where(ids_by_row(d) == lane_id, 1.0, 0.0).astype(BF16)
        for h, key in enumerate(split_heads(ks.at[d])):
            kx[h, :, 0:hd] = key.astype(BF16)
            kx[h, :, hd:] = match

    def prepare_values(d):
        for h, value in enumerate(split_heads(vs.at[d])):
            vt[h, 0:hd, :] = value.T.astype(BF16)

    def attend(d, h, part="all"):
        def extent(t):
            low, high = 0, rows
            if d == 0:
                high = min(rows, (t + 1) * tile_pos)
            elif d == window:
                low = t * tile_pos // 16 * 16
            return low, high

        def scores(t):
            low, high = extent(t)
            got = lax.dot_general(kx[h, low:high, :], qs[h, t * TILE:(t + 1) * TILE, :],
                                  (((1,), (1,)), ((), ())), preferred_element_type=F32)
            if d == 0:
                key_pos = lax.broadcasted_iota(jnp.int32, (high - low, TILE), 0)
                query_pos = (t * TILE + lax.broadcasted_iota(jnp.int32, (1, TILE), 1)) // group
                got = jnp.where(key_pos <= query_pos, got, HIDE)
            held[t % 4, low:high, :] = got
            return jnp.max(got, axis=0, keepdims=True)

        def tile(t, top):
            low, high = extent(t)
            cols = slice(t * TILE, (t + 1) * TILE)
            first, last = low // 128 * 128, -(-high // 128) * 128
            if part == "values":
                new = jnp.dot(vt[h, :, first:last], later[h, first:last, cols], preferred_element_type=F32)
                acc[h, :, cols] = new + acc[h, :, cols] * shrink[h, 0:1, cols]
                return
            if d > 0:
                old = mstat[h, 0:1, cols]
                top = jnp.maximum(old, top)
            p = jnp.exp2((held[t % 4, low:high, :] - top) * factor).astype(BF16)
            parts = [p]
            if low > first:
                parts = [jnp.zeros((low - first, TILE), BF16)] + parts
            if last > high:
                parts = parts + [jnp.zeros((last - high, TILE), BF16)]
            p = jnp.concatenate(parts, axis=0) if len(parts) > 1 else p
            if part == "keys":
                later[h, first:last, cols] = p
                shrink[h, :, cols] = jnp.broadcast_to(jnp.exp2((old - top) * factor), (8, TILE))
                mstat[h, :, cols] = jnp.broadcast_to(top, (8, TILE))
                return
            new = jnp.dot(vt[h, :, first:last], p, preferred_element_type=F32)
            if d > 0:
                new = new + acc[h, :, cols] * jnp.exp2((old - top) * factor)
            acc[h, :, cols] = new
            mstat[h, :, cols] = jnp.broadcast_to(top, (8, TILE))

        tiles = flat // TILE
        if part == "values":
            for t in range(tiles):
                tile(t, None)
            return
        ready = [scores(t) for t in range(min(3, tiles))]
        for t in range(tiles):
            if t + 3 < tiles:
                ready.append(scores(t + 3))
            tile(t, ready[t])

    def wait_rest(d, some):
        if d % 2 == 0 and d // 2 < half:
            return
        for j in some:
            if d % 2 == 0:
                @pl.when(is_odd == 0)
                def _():
                    wait_piece(d, j)
            else:
                wait_piece(d, j)

    def when_held(d, act, *args):
        @pl.when(c >= d)
        def _():
            act(*args)

    def forwards(k, some):
        if k <= half:
            for j in some:
                forward(k, j)

    def take_keys(d):
        wait_rest(d, range(1 + PARTS))
        prepare_keys(d)

    def take_values(d):
        wait_rest(d, range(1 + PARTS, chunks))
        if d == 2 * half - 3:
            detours(lambda j, copy: copy.start())
        prepare_values(d)

    loads[2].wait()
    loads[3].wait()
    prepare_keys(0)
    prepare_values(0)
    attend(0, 0)
    forwards(1, range(2))
    for h in range(1, heads):
        attend(0, h)
    ahead = 2
    for k in range(1, half + 1):
        forwards(k, range(ahead, 1 + PARTS))
        due = [range(1 + PARTS, 1 + PARTS + PARTS // 2), range(1 + PARTS + PARTS // 2, chunks)]
        when_held(2 * k, take_keys, 2 * k)
        for h in range(heads):
            when_held(2 * k, attend, 2 * k, h, "keys")
            if h < 2:
                forwards(k, due[h])
        when_held(2 * k, take_values, 2 * k)
        for h in range(heads):
            when_held(2 * k, attend, 2 * k, h, "values")
        d = 2 * k - 1
        when_held(d, take_keys, d)
        for h in range(heads):
            when_held(d, attend, d, h, "keys")
            if h == 0:
                forwards(k + 1, range(ahead))
        when_held(d, take_values, d)
        for h in range(heads):
            when_held(d, attend, d, h, "values")

    def sub_id(width):
        return lax.broadcasted_iota(jnp.int32, (8, width), 0)

    pieces = flat // spread_rows
    lines = []
    for t in range(flat // TILE):
        cols = slice(t * TILE, (t + 1) * TILE)
        line = jnp.zeros((1, TILE), F32)
        for h in range(heads):
            got = (acc[h, 0:hd, cols] * (1.0 / acc[h, hd:hd + 1, cols])).astype(BF16)
            done[h, :, cols] = got
            line = line + jnp.sum(got.astype(F32) * swt[h], axis=0, keepdims=True)
        lines.append(line)
    for p in range(pieces):
        span = spread_rows // TILE
        line = jnp.concatenate(lines[p * span:(p + 1) * span], axis=1)
        high = line.astype(BF16).astype(F32)
        middle = (line - high).astype(BF16).astype(F32)
        low = line - high - middle
        three = jnp.where(sub_id(spread_rows) == 0, high, jnp.where(sub_id(spread_rows) == 1, middle, jnp.where(sub_id(spread_rows) == 2, low, 0.0)))
        got = jnp.dot(three.astype(BF16), spread[...], preferred_element_type=F32)
        part[:, p * 128:(p + 1) * 128] = jnp.sum(got, axis=0, keepdims=True)
    share = pltpu.make_async_remote_copy(
        src_ref=part, dst_ref=part_in, send_sem=score_sem.at[0], recv_sem=score_sem.at[1],
        device_id={"head": 1 - hc}, device_id_type=MESH)
    share.start()
    for t in range(flat // TILE):
        for h in range(heads):
            got = done[h, :, t * TILE:(t + 1) * TILE].astype(F32).T
            out_ref[t * tile_pos:(t + 1) * tile_pos, h] = got.reshape(tile_pos, group, hd).astype(BF16)
    for k in range(half + 1):
        for j in range(chunks):
            sends(k, j, lambda copy: copy.wait_send())
    detours(lambda j, copy: copy.wait_send())
    share.wait()
    score_ref[...] = part[...] + part_in[...]


def put_out(attended_ref, score_ref, attended_out, score_out, sem):
    rows = attended_ref.shape[0] // OUTS
    copies = [pltpu.make_async_copy(score_ref, score_out, sem.at[OUTS])]
    for i in range(OUTS):
        span = pl.ds(i * rows, rows)
        copies.append(pltpu.make_async_copy(attended_ref.at[span], attended_out.at[span], sem.at[i]))
    for copy in copies:
        copy.start()
    for copy in copies:
        copy.wait()


def local(n, queries, keys, values, segments, score_weight):
    rows, heads, group, hd = queries.shape
    window = max(2, n // 2)
    flat = rows * group
    chunks = 1 + 2 * PARTS
    anywhere = pl.BlockSpec(memory_space=pl.ANY)
    vmem = pl.BlockSpec(memory_space=pltpu.VMEM)
    attended, score = pl.pallas_call(
        functools.partial(kernel, n, window),
        out_shape=(
            pltpu.VMEM(queries.shape, BF16),
            pltpu.VMEM((1, rows), F32),
        ),
        in_specs=[anywhere] * 5,
        out_specs=(vmem, vmem),
        scratch_shapes=[
            pltpu.VMEM((window + 1, rows * heads, hd), BF16),
            pltpu.VMEM((window + 1, rows * heads, hd), BF16),
            pltpu.VMEM((window + 1, 1, rows), jnp.int32),
            pltpu.VMEM(queries.shape, BF16),
            pltpu.VMEM(score_weight.shape, BF16),
            pltpu.VMEM((rows * heads, hd), F32),
            pltpu.VMEM((heads, flat, 2 * hd), BF16),
            pltpu.VMEM((heads, rows, 2 * hd), BF16),
            pltpu.VMEM((4, rows, TILE), F32),
            pltpu.VMEM((heads, hd + PAD, flat), F32),
            pltpu.VMEM((heads, 8, flat), F32),
            pltpu.VMEM((heads, hd + PAD, rows), BF16),
            pltpu.VMEM((heads, hd, TILE), F32),
            pltpu.VMEM((128 * group, 128), BF16),
            pltpu.VMEM((heads, rows, flat), BF16),
            pltpu.VMEM((heads, 8, flat), F32),
            pltpu.VMEM((heads, hd, flat), BF16),
            pltpu.VMEM((1, rows), F32),
            pltpu.VMEM((1, rows), F32),
            pltpu.SemaphoreType.DMA((5,)),
            pltpu.SemaphoreType.DMA((window // 2, chunks)),
            pltpu.SemaphoreType.DMA((window // 2 + 1, chunks)),
            pltpu.SemaphoreType.DMA((max(1, DETOUR),)),
            pltpu.SemaphoreType.DMA((window, chunks)),
            pltpu.SemaphoreType.DMA((2,)),
        ],
        compiler_params=pltpu.CompilerParams(collective_id=0, has_side_effects=True),
    )(queries, keys.reshape(rows * heads, hd), values.reshape(rows * heads, hd), segments.reshape(1, rows), score_weight)
    attended, score = pl.pallas_call(
        put_out,
        out_shape=(jax.ShapeDtypeStruct(attended.shape, BF16), jax.ShapeDtypeStruct(score.shape, F32)),
        in_specs=[vmem] * 2,
        out_specs=(anywhere, anywhere),
        scratch_shapes=[pltpu.SemaphoreType.DMA((OUTS + 1,))],
    )(pltpu.with_memory_space_constraint(attended, pltpu.VMEM), pltpu.with_memory_space_constraint(score, pltpu.VMEM))
    return attended, score.reshape(rows)


def solution(mesh):
    return jax.shard_map(
        functools.partial(local, mesh.shape["ctx"]),
        mesh=mesh,
        in_specs=(
            P(("groups", "ctx"), "head", None, None),
            P(("groups", "ctx"), "head", None),
            P(("groups", "ctx"), "head", None),
            P(("groups", "ctx")),
            P("head", None, None),
        ),
        out_specs=(P(("groups", "ctx"), "head", None, None), P(("groups", "ctx"))),
        check_vma=False,
    )
```
